32 devices in a mesh: energy: 8 (over y, x, core), slab: 4 (over z).
Axes of the slice: x: 2, y: 2, z: 4, core: 2. Of those that a mesh axis runs over, the one named last changes fastest.
Arguments:
- green_rows: float32 [2, 16, 1024, 512], P(None, 'energy', 'slab'), may hold values from -6 to 6
- less_surfaces: float32 [2, 16, 1024, 128], P(None, 'energy', 'slab'), may hold values from -6 to 6
- less_diag: float32 [2, 16, 2048], P(None, 'energy', 'slab'), may hold values from -6 to 6
- neighbours: int32 [4, 2, 8, 512], P('slab'), may hold values from 0 to 127
- hopping: float32 [4, 2, 8, 512], P('slab'), may hold values from -0.046875 to 0.046875
- damp: float32 [4, 512], P('slab'), may hold values from 0 to 1
- mode_offset: int32 [8], replicated, may hold values from 1 to 8, as said below
- mode_strength: float32 [8], replicated, may hold values from 0.002 to 0.02
- bose: float32 [8], replicated, may hold values from 0.05 to 2
Outputs:
- correction: float32 [2, 16, 1024, 128], P(None, 'energy', 'slab')
- self_energy: float32 [2, 16, 2048], P(None, 'energy', 'slab')
The draws below stay inside these ranges and needn't reach their ends.
Inputs may be any that keep to these rules, and one draw needn't show every extreme that they name: `neighbours`: a position within the facing surface of the adjacent slab. `mode_offset`: some mode has offset exactly 8.
All inputs are finite; a program needn't handle non-finite values.
Results may differ from the reference program's by a relative error of at most 0.000071.
Values sent between devices are 32-bit elements; how exact they have to be, the bound alone decides.
No kernel may reach another device: no remote copies, remote signals or barrier semaphores. Data moves between devices by JAX's collectives and lax.ppermute only.
A program may use at most 64 MiB of HBM per device.

```python
import math
import jax
import jax.numpy as jnp
from jax import lax

SLAB_ORBITALS = 512
SURF = 128
NB = 8
MODES = 8
ENERGIES = 16
SLAB_TOTAL = 4
SPAN = 8


def draw_damp(key, part):
    rate_key, slab_key, place_key, depth_random_key = jax.random.split(jax.random.fold_in(key, 17), 4)
    low_end = 0.05
    high_end = 30.0
    decay_rate = jnp.exp(jax.random.uniform(rate_key, (1, SLAB_ORBITALS), jnp.float32, math.log(low_end), math.log(high_end)))
    factor = jnp.exp(jax.random.uniform(slab_key, (SLAB_TOTAL, SLAB_ORBITALS), jnp.float32, math.log(0.5), math.log(2.0)))
    slab_entries = jnp.exp(-decay_rate * factor / SLAB_TOTAL)
    slab_locations = jax.random.randint(place_key, (2,), 0, SLAB_TOTAL)
    slab_indices = lax.broadcasted_iota(jnp.int32, (SLAB_TOTAL, 1), 0)
    pulse_groups = jnp.any(slab_indices == slab_locations[None, :], axis=1, keepdims=True)
    pulse_depth = jax.random.uniform(depth_random_key, (SLAB_TOTAL, SLAB_ORBITALS), jnp.float32, 0.5, 0.8)
    return jnp.where(pulse_groups, slab_entries * pulse_depth, slab_entries).astype(jnp.float32)


def draw_mode_offset(key, part):
    value_key, which_key = jax.random.split(jax.random.fold_in(key, 29), 2)
    offsets = jax.random.randint(value_key, (MODES,), 1, SPAN + 1)
    chosen = jax.random.randint(which_key, (), 0, MODES)
    mode_ids = lax.broadcasted_iota(jnp.int32, (MODES,), 0)
    return jnp.where(mode_ids == chosen, SPAN, offsets).astype(jnp.int32)


def touch_ends(values, stream_key, least, largest):
    place = [jax.random.randint(jax.random.fold_in(stream_key, axis), (), 0, length) for axis, length in enumerate(values.shape)]
    widest = values.shape.index(max(values.shape))
    next_to = place[:widest] + [(place[widest] + 1) % values.shape[widest]] + place[widest + 1:]
    return values.at[tuple(place)].set(least).at[tuple(next_to)].set(largest)


def block_scale(own_key, dims, cuts, least, high):
    factor_of, own = 1.0, jax.random.fold_in(own_key, 6)
    for dim, shards_of in cuts:
        draws = jnp.exp(jax.random.uniform(jax.random.fold_in(own, dim), (shards_of,), jnp.float32, least / len(cuts), high / len(cuts)))
        factor_of = factor_of * jnp.repeat(draws, dims[dim] // shards_of).reshape([-1 if axis == dim else 1 for axis in range(len(dims))])
    return factor_of


def scatter_about(own_key, dims, width, most, cuts=(), kind=jnp.bfloat16):
    level = block_scale(own_key, dims, cuts, -0.22, 0.18) if cuts else 1.0
    array = jax.random.normal(own_key, dims, jnp.float32) * width * level
    return jnp.minimum(jnp.maximum(array, -most), most).astype(kind)


def setup_inputs(seed: int = 0) -> dict:
    key_list = jax.random.split(jax.random.key(seed), 10)
    green_rows = scatter_about(key_list[0], (2, ENERGIES, SLAB_TOTAL * 2 * SURF, SLAB_ORBITALS), 1.0, 6.0, ((1, 8), (2, 4)), jnp.float32)
    less_surfaces = scatter_about(key_list[1], (2, ENERGIES, SLAB_TOTAL * 2 * SURF, SURF), 1.0, 6.0, ((1, 8), (2, 4)), jnp.float32)
    less_diag = scatter_about(key_list[2], (2, ENERGIES, SLAB_TOTAL * SLAB_ORBITALS), 1.0, 6.0, ((1, 8), (2, 4)), jnp.float32)
    neighbours = touch_ends(jax.random.randint(key_list[3], (SLAB_TOTAL, 2, NB, SLAB_ORBITALS), 0, SURF), jax.random.fold_in(key_list[3], 1), 0, SURF - 1).astype(jnp.int32)
    hopping = scatter_about(key_list[4], (SLAB_TOTAL, 2, NB, SLAB_ORBITALS), (SLAB_ORBITALS * NB * 4) ** -0.5, 0.046875, ((0, 4),), jnp.float32)
    damp = draw_damp(jax.random.fold_in(key_list[9], 71), 0)
    mode_offset = draw_mode_offset(jax.random.fold_in(key_list[9], 71), 0)
    mode_strength = jnp.clip(jnp.exp(jax.random.uniform(key_list[7], (MODES,), jnp.float32, math.log(0.002), math.log(0.02))), 0.002, 0.02)
    bose = jnp.clip(jnp.exp(jax.random.uniform(key_list[8], (MODES,), jnp.float32, math.log(0.05), math.log(2.0))), 0.05, 2.0)
    return dict(green_rows=green_rows, less_surfaces=less_surfaces, less_diag=less_diag, neighbours=neighbours, hopping=hopping, damp=damp, mode_offset=mode_offset, mode_strength=mode_strength, bose=bose)


PRECISE = lax.Precision.HIGHEST


def coupling_blocks(neighbours, hopping):
    slot_ids = lax.broadcasted_iota(jnp.int32, (1, 1, 1, SURF, 1), 3)
    one_hot = (neighbours[:, :, :, None, :] == slot_ids).astype(jnp.float32)
    return jnp.sum(one_hot * hopping[:, :, :, None, :], axis=2)


def phonon_kernel(mode_offset, mode_strength, bose, energy_count):
    row_ids = lax.broadcasted_iota(jnp.int32, (1, energy_count, energy_count), 1)
    column_ids = lax.broadcasted_iota(jnp.int32, (1, energy_count, energy_count), 2)
    shifts = mode_offset[:, None, None]
    emitted = (column_ids == row_ids + shifts).astype(jnp.float32)
    absorbed = (column_ids == row_ids - shifts).astype(jnp.float32)
    occupied = bose[:, None, None]
    return jnp.sum(mode_strength[:, None, None] * ((occupied + 1.0) * emitted + occupied * absorbed), axis=0)


def complex_product(left_factor, right_factor, pattern):
    real_part = jnp.einsum(pattern, left_factor[0], right_factor[0], precision=PRECISE) - jnp.einsum(pattern, left_factor[1], right_factor[1], precision=PRECISE)
    imag_part = jnp.einsum(pattern, left_factor[0], right_factor[1], precision=PRECISE) + jnp.einsum(pattern, left_factor[1], right_factor[0], precision=PRECISE)
    return jnp.stack([real_part, imag_part])


def block_outer(left_factor, right_factor, surface):
    shape_in = left_factor.shape
    block_count = shape_in[2] // surface
    left_blocks = left_factor.reshape(shape_in[0], shape_in[1], block_count, surface, shape_in[3])
    right_blocks = right_factor.reshape(shape_in[0], shape_in[1], block_count, surface, shape_in[3])
    pattern = "abik,abjk->abij"
    real_part = jnp.einsum(pattern, left_blocks[0], right_blocks[0], precision=PRECISE) + jnp.einsum(pattern, left_blocks[1], right_blocks[1], precision=PRECISE)
    imag_part = jnp.einsum(pattern, left_blocks[1], right_blocks[0], precision=PRECISE) - jnp.einsum(pattern, left_blocks[0], right_blocks[1], precision=PRECISE)
    return jnp.stack([real_part, imag_part]).reshape(shape_in[0], shape_in[1], shape_in[2], surface)


def reference(green_rows, less_surfaces, less_diag, neighbours, hopping, damp, mode_offset, mode_strength, bose):
    couple = coupling_blocks(neighbours, hopping)
    diagonals = less_diag.reshape(2, ENERGIES, SLAB_TOTAL, SLAB_ORBITALS)

    def advance(carried_state, operands):
        rate_row, local_terms = operands
        return rate_row * carried_state + local_terms, carried_state

    final_state, carried = lax.scan(advance, jnp.zeros((2, ENERGIES, SLAB_ORBITALS), jnp.float32), (damp, jnp.moveaxis(diagonals, 2, 0)))
    occupation = diagonals + jnp.moveaxis(carried, 0, 2)
    kernel = phonon_kernel(mode_offset, mode_strength, bose, ENERGIES)
    phonon_sigma = jnp.einsum("ef,cfso->ceso", kernel, occupation, precision=PRECISE)
    surfaces = less_surfaces.reshape(2, ENERGIES, SLAB_TOTAL, 2, SURF, SURF)
    zero_block = jnp.zeros((2, ENERGIES, 1, SURF, SURF), jnp.float32)
    from_lower = jnp.concatenate([zero_block, surfaces[:, :, :-1, 1]], axis=2)
    from_upper = jnp.concatenate([surfaces[:, :, 1:, 0], zero_block], axis=2)
    greens = green_rows.reshape(2, ENERGIES, SLAB_TOTAL, 2 * SURF, SLAB_ORBITALS)

    def one_energy(operands):
        green_now, lower_now, upper_now, sigma_now = operands
        coupled_lower = jnp.einsum("csrj,sqj->csrq", green_now, couple[:, 0], precision=PRECISE)
        coupled_upper = jnp.einsum("csrj,sqj->csrq", green_now, couple[:, 1], precision=PRECISE)
        weighted_lower = complex_product(coupled_lower, lower_now, "srq,sqt->srt")
        weighted_upper = complex_product(coupled_upper, upper_now, "srq,sqt->srt")
        scaled = jnp.stack([
            green_now[0] * sigma_now[0][:, None, :] - green_now[1] * sigma_now[1][:, None, :],
            green_now[0] * sigma_now[1][:, None, :] + green_now[1] * sigma_now[0][:, None, :]])
        left_side = jnp.concatenate([scaled, weighted_lower, weighted_upper], axis=3)
        right_side = jnp.concatenate([green_now, coupled_lower, coupled_upper], axis=3)
        return block_outer(left_side, right_side, SURF)

    per_energy = (jnp.moveaxis(greens, 1, 0), jnp.moveaxis(from_lower, 1, 0), jnp.moveaxis(from_upper, 1, 0), jnp.moveaxis(phonon_sigma, 1, 0))
    blocks = lax.map(one_energy, per_energy)
    correction = jnp.moveaxis(blocks, 0, 1).reshape(2, ENERGIES, SLAB_TOTAL * 2 * SURF, SURF)
    return correction, phonon_sigma.reshape(2, ENERGIES, SLAB_TOTAL * SLAB_ORBITALS)
```

```python
import functools

import jax
import jax.numpy as jnp
from jax import lax
from jax.experimental import pallas as pl
from jax.experimental.pallas import tpu as pltpu
from jax.sharding import PartitionSpec as P

AXES = ("energy", "slab")
F32, BF16 = jnp.float32, jnp.bfloat16


def swap(value, target):
    energies, slabs = lax.axis_size("energy"), lax.axis_size("slab")
    pairs = []
    for e in range(energies):
        for s in range(slabs):
            to_e, to_s = target(e, s)
            pairs.append((e * slabs + s, to_e * slabs + to_s))
    return lax.ppermute(value, AXES, pairs)


def split(value):
    high = value.astype(BF16)
    return high, (value - high.astype(F32)).astype(BF16)


NT = (((1,), (1,)), ((), ()))
NN = (((1,), (0,)), ((), ()))


def product(left, right, dims):
    dot = functools.partial(lax.dot_general, dimension_numbers=dims, preferred_element_type=F32)
    return dot(left[0], right[0]) + (dot(left[0], right[1]) + dot(left[1], right[0]))


def join(parts, axis):
    return [jnp.concatenate([p[i] for p in parts], axis=axis) for i in range(2)]


def prepare_kernel(surfaces, diag, damp, first, second, diag_out, damp_out, sems):
    rows, surface = surfaces.shape[2], first.shape[2]
    shift = (rows - surface) * (lax.axis_index("slab") % 2)
    upper = pl.multiple_of(rows - surface - shift, surface)
    lower = pl.multiple_of(shift, surface)
    copies = [
        pltpu.make_async_copy(surfaces.at[:, :, pl.ds(upper, surface)], first, sems.at[0]),
        pltpu.make_async_copy(surfaces.at[:, :, pl.ds(lower, surface)], second, sems.at[1]),
        pltpu.make_async_copy(diag, diag_out, sems.at[2]),
        pltpu.make_async_copy(damp, damp_out, sems.at[3]),
    ]
    for copy in copies:
        copy.start()
    for copy in copies:
        copy.wait()


def pack_kernel(mine, other, damp, message):
    comps, energies, orbitals = mine.shape
    core = lax.axis_index("energy") % 2
    for c in range(comps):
        at = c * 2 * energies
        message[at : at + energies, :] = jnp.where(core == 0, mine[c], other[c])
        message[at + energies : at + 2 * energies, :] = jnp.where(core == 0, other[c], mine[c])
    message[comps * 2 * energies :, :] = damp[...]


def combine_kernel(bit, size, last, *refs):
    got, refs = refs[:size], refs[size:]
    state, outs = (refs[:3], refs[3:]) if bit > 1 else ((), refs)
    place = (lax.axis_index("slab") // bit) % size
    count = got[0].shape[0] - 1
    pieces = [(g[:count], g[count:]) for g in got]
    shape = pieces[0][0].shape
    before, span = jnp.zeros(shape, F32), jnp.ones(pieces[0][1].shape, F32)
    total, through = before, span
    for m in range(size):
        value, decay = pieces[0]
        for k in range(1, size):
            value = jnp.where((place ^ m) == k, pieces[k][0], value)
            decay = jnp.where((place ^ m) == k, pieces[k][1], decay)
        before = jnp.where(m < place, decay * before + value, before)
        span = jnp.where(m < place, decay * span, span)
        total, through = decay * total + value, decay * through
    start = pieces[0][0]
    if bit > 1:
        start = state[0][...]
        before = state[2][...] * before + state[1][...]
        span = state[2][...] * span
    if last:
        outs[0][...] = start + before
    else:
        outs[0][...] = start
        outs[1][...] = before
        outs[2][...] = span
        outs[3][:count, :] = total
        outs[3][count:, :] = through


def coupled_kernel(
    chips, green, near_in, hop_in, offset_in, strength_in, bose_in,
    g, g_hi, g_lo, c_hi, c_lo, weight,
    near, hop, offset, strength, bose, sems,
):
    comps, energies, rows, orbitals = green.shape
    surface = c_hi.shape[3] // 2
    small = [
        pltpu.make_async_copy(source, target, sems.at[n])
        for n, (source, target) in enumerate(
            ((near_in, near), (hop_in, hop), (offset_in, offset), (strength_in, strength), (bose_in, bose))
        )
    ]
    large = [
        pltpu.make_async_copy(green.at[c, e], g.at[c, e], sems.at[5 + c * energies + e])
        for c in range(comps)
        for e in range(energies)
    ]
    for copy in small + large:
        copy.start()
    small[0].wait()
    small[1].wait()
    ids = lax.broadcasted_iota(jnp.int32, (surface, orbitals), 0)
    sides = []
    for t in range(2):
        total = jnp.zeros((surface, orbitals), F32)
        for k in range(near.shape[2]):
            total += jnp.where(near[0, t, k : k + 1, :] == ids, hop[0, t, k : k + 1, :], 0.0)
        sides.append(total)
    couple = split(jnp.concatenate(sides, axis=0))
    for c in range(comps):
        for e in range(energies):
            large[c * energies + e].wait()
            green_now = split(g[c, e])
            g_hi[c, e], g_lo[c, e] = green_now
            c_hi[c, e], c_lo[c, e] = split(product(green_now, couple, NT))
    for copy in small[2:]:
        copy.wait()
    me = lax.axis_index("energy")
    chip, first, per_chip = me // 2, me * energies, 2 * energies
    row = lax.broadcasted_iota(jnp.int32, weight.shape[2:], 0)
    source = (chip ^ (row // (comps * per_chip))) * per_chip + row % per_chip
    part = (row // per_chip) % comps
    for i in range(energies):
        step = source - (first + i)
        total = jnp.zeros(weight.shape[2:], F32)
        for q in range(offset.shape[0]):
            gain = (bose[q] + 1.0) * (step == offset[q]).astype(F32)
            loss = bose[q] * (step == -offset[q]).astype(F32)
            total += strength[q] * (gain + loss)
        for c in range(comps):
            weight[c, i] = jnp.where(part == c, total, 0.0)


def boundary_kernel(slabs, c_hi, c_lo, first, second, out):
    comps, energies, rows, both = c_hi.shape
    surface = both // 2
    slab = lax.axis_index("slab")
    even, has_low, has_up = slab % 2 == 0, slab > 0, slab < slabs - 1
    for e in range(energies):
        coupled = [[c[0, e], c[1, e]] for c in (c_hi, c_lo)]
        sides = []
        for t, valid in ((0, has_low), (1, has_up)):
            pick = even if t == 1 else jnp.logical_not(even)
            use_first = jnp.logical_and(valid, pick)
            use_second = jnp.logical_and(valid, jnp.logical_not(pick))
            real, imag = [
                jnp.where(use_first, first[c, e], jnp.where(use_second, second[c, e], 0.0))
                for c in range(2)
            ]
            right = jnp.concatenate(
                [jnp.concatenate([real, imag], 1), jnp.concatenate([-imag, real], 1)], 0
            )
            left = [
                jnp.concatenate([p[:, t * surface : (t + 1) * surface] for p in parts], 1)
                for parts in coupled
            ]
            sides.append(product(left, split(right), NN))
        low, up = sides
        w_real = jnp.concatenate([low[:, :surface], up[:, :surface]], 1)
        w_imag = jnp.concatenate([low[:, surface:], up[:, surface:]], 1)
        for b in range(rows // surface):
            at = slice(b * surface, (b + 1) * surface)
            left = split(jnp.concatenate([w_real[at], w_imag[at]], 0))
            right = [jnp.concatenate([parts[0][at], parts[1][at]], 0) for parts in coupled]
            full = product(left, right, NT)
            out[0, e, at, :] = full[:surface, :surface] + full[surface:, surface:]
            out[1, e, at, :] = full[surface:, :surface] - full[:surface, surface:]


def final_kernel(g, g_hi, g_lo, weight, edge, *rest):
    pieces, (out_hbm, sigma_hbm, out, sigma_out, sems) = rest[:-5], rest[-5:]
    comps, energies, rows, orbitals = g_hi.shape
    surface = out.shape[3]
    lanes = weight.shape[3]
    occupied = jnp.concatenate([p[...] for p in pieces], axis=0)
    sigma = []
    for c in range(comps):
        for i in range(energies):
            w = jnp.concatenate([weight[c, i]] * (orbitals // lanes), axis=1)
            row = jnp.sum(occupied * w, axis=0, keepdims=True)
            sigma.append(row)
            sigma_out[c, i : i + 1, :] = row
    copies = [pltpu.make_async_copy(sigma_out, sigma_hbm, sems.at[0])]
    copies[0].start()
    for e in range(energies):
        s_real, s_imag = sigma[e], sigma[energies + e]
        for b in range(rows // surface):
            at = slice(b * surface, (b + 1) * surface)
            right = [jnp.concatenate([h[0, e, at], h[1, e, at]], 0) for h in (g_hi, g_lo)]
            real, imag = g[0, e, at], g[1, e, at]
            left = split(
                jnp.concatenate(
                    [real * s_real - imag * s_imag, real * s_imag + imag * s_real], 0
                )
            )
            full = product(left, right, NT)
            out[0, e, at, :] = edge[0, e, at, :] + (
                full[:surface, :surface] + full[surface:, surface:]
            )
            out[1, e, at, :] = edge[1, e, at, :] + (
                full[surface:, :surface] - full[:surface, surface:]
            )
            copies.append(
                pltpu.make_async_copy(
                    out.at[:, e, at], out_hbm.at[:, e, at], sems.at[len(copies)]
                )
            )
            copies[-1].start()
    for copy in copies:
        copy.wait()


VMEM = pl.BlockSpec(memory_space=pltpu.VMEM)
HBM = pl.BlockSpec(memory_space=pltpu.HBM)


def call(kernel, arrays, outs, flops, name, sources=VMEM, targets=VMEM, scratch=()):
    moved = sum(a.size * a.dtype.itemsize for a in arrays) + sum(
        o.size * o.dtype.itemsize for o in outs
    )
    if sources is HBM:
        arrays = [pltpu.with_memory_space_constraint(a, pltpu.HBM) for a in arrays]
    return pl.pallas_call(
        kernel,
        out_shape=outs,
        in_specs=[sources] * len(arrays),
        out_specs=[targets] * len(outs),
        scratch_shapes=scratch,
        cost_estimate=pl.CostEstimate(flops=flops, bytes_accessed=moved, transcendentals=0),
        compiler_params=pltpu.CompilerParams(vmem_limit_bytes=12 * 2**20),
        name=name,
    )(*arrays)


def rounds(count):
    bit, out = 1, []
    while bit < count:
        size = min(4, count // bit)
        out.append((bit, size))
        bit *= size
    return out


def local(
    green_rows,
    less_surfaces,
    less_diag,
    neighbours,
    hopping,
    damp,
    mode_offset,
    mode_strength,
    bose,
):
    comps, energies, rows, orbitals = green_rows.shape
    surface = less_surfaces.shape[3]
    devices, slabs = lax.axis_size("energy"), lax.axis_size("slab")
    chips, per_chip = devices // 2, 2 * energies
    shape, dma = jax.ShapeDtypeStruct, pltpu.SemaphoreType.DMA
    half = (comps, energies, surface, surface)
    work = comps * energies * rows

    other = swap(less_diag, lambda e, s: (e ^ 1, s))
    first, second, diag, decay = call(
        prepare_kernel,
        (less_surfaces, less_diag, damp),
        [shape(half, F32), shape(half, F32), shape(less_diag.shape, F32), shape(damp.shape, F32)],
        0,
        "prepare",
        sources=HBM,
        scratch=[dma((4,))],
    )
    first = swap(first, lambda e, s: (e, s ^ 1))

    def across(e, s):
        to = ((s + 1) ^ 1) - 1
        return (e, to) if 0 <= to < slabs else (e ^ 1, s)

    second = swap(second, across)

    count = comps * per_chip
    rowed = shape((count, orbitals), F32)
    letter = shape((count + 1, orbitals), F32)
    (message,) = call(pack_kernel, (diag, other, decay), [letter], 0, "pack")
    state = ()
    for bit, size in rounds(slabs):
        got = [message] + [
            swap(message, lambda e, s, k=k * bit: (e ^ 1, s ^ k)) for k in range(size - 1, 0, -1)
        ]
        got = [got[0]] + got[:0:-1]
        last = bit * size >= slabs
        outs = [rowed] if last else [rowed, rowed, shape(decay.shape, F32), letter]
        result = call(
            functools.partial(combine_kernel, bit, size, last), (*got, *state), outs, 0, "combine"
        )
        state, message = result[:3], result[-1]

    pieces = [message]
    for bit, size in rounds(chips):
        block = jnp.concatenate(pieces, axis=0) if len(pieces) > 1 else pieces[0]
        pieces = [block] + [
            swap(block, lambda e, s, k=k * bit: (e ^ 1 ^ (2 * k), s)) for k in range(1, size)
        ]

    pair = (comps, energies, rows, 2 * surface)
    smem = pltpu.SMEM
    g, g_hi, g_lo, c_hi, c_lo, weight = call(
        functools.partial(coupled_kernel, chips),
        (green_rows, neighbours, hopping, mode_offset, mode_strength, bose),
        [
            shape(green_rows.shape, F32),
            shape(green_rows.shape, BF16),
            shape(green_rows.shape, BF16),
            shape(pair, BF16),
            shape(pair, BF16),
            shape((comps, energies, chips * count, 128), F32),
        ],
        6 * work * orbitals * 2 * surface,
        "coupled",
        sources=HBM,
        scratch=[
            pltpu.VMEM(neighbours.shape, jnp.int32),
            pltpu.VMEM(hopping.shape, F32),
            smem(mode_offset.shape, jnp.int32),
            smem(mode_strength.shape, F32),
            smem(bose.shape, F32),
            dma((5 + comps * energies,)),
        ],
    )
    (edge,) = call(
        functools.partial(boundary_kernel, slabs),
        (c_hi, c_lo, first, second),
        [shape(less_surfaces.shape, F32)],
        12 * work * 2 * surface * 2 * surface,
        "boundary",
    )
    return call(
        final_kernel,
        (g, g_hi, g_lo, weight, edge, *pieces),
        [shape(less_surfaces.shape, F32), shape(less_diag.shape, F32)],
        12 * work * orbitals * surface,
        "final",
        targets=HBM,
        scratch=[
            pltpu.VMEM(less_surfaces.shape, F32),
            pltpu.VMEM(less_diag.shape, F32),
            dma((1 + energies * (rows // surface),)),
        ],
    )


def solution(mesh):
    placed = (
        P(None, "energy", "slab", None),
        P(None, "energy", "slab", None),
        P(None, "energy", "slab"),
        P("slab", None, None, None),
        P("slab", None, None, None),
        P("slab", None),
        P(),
        P(),
        P(),
    )

    def step(*arrays):
        out, sigma = local(*arrays)
        return out, sigma

    return jax.shard_map(
        step,
        mesh=mesh,
        in_specs=placed,
        out_specs=(P(None, "energy", "slab", None), P(None, "energy", "slab")),
        check_vma=False,
    )
```
